32 devices in a mesh: seq: 4 (over z), head: 2 (over y), dp: 4 (over x, core).
Axes of the slice: x: 2, y: 2, z: 4, core: 2. Of those that a mesh axis runs over, the one named last changes fastest.
Arguments:
- layer_input: bfloat16 [4, 512, 6144], P('dp', 'seq'), may hold values from -6 to 6
- queries: bfloat16 [4, 512, 1024], P('dp', 'seq', 'head'), may hold values from -6 to 6
- key_rows: bfloat16 [4, 512, 1024], P('dp', 'seq', 'head'), may hold values from -6 to 6
- value_rows: bfloat16 [4, 512, 1024], P('dp', 'seq', 'head'), may hold values from -6 to 6
- grad_out: bfloat16 [4, 512, 1024], P('dp', 'seq', 'head'), may hold values from -6 to 6
- log_decay: float32 [4, 512, 8], P('dp', 'seq', 'head'), may hold values from -2 to 0, as said below
Outputs:
- grad_query: bfloat16 [4, 512, 1024], P('dp', 'seq', 'head')
- grad_key: bfloat16 [4, 512, 1024], P('dp', 'seq', 'head')
- grad_value: bfloat16 [4, 512, 1024], P('dp', 'seq', 'head')
- key_weight_grad: bfloat16 [6144, 1024], P('seq', 'head')
- value_weight_grad: bfloat16 [6144, 1024], P('seq', 'head')
The draws below stay inside these ranges and needn't reach their ends.
Inputs may be any that keep to these rules, and one draw needn't show every extreme that they name: log_decay is never positive.
All inputs are finite; a program needn't handle non-finite values.
Results may differ from the reference program's by a relative error of at most 0.0062.
Values may be sent and summed in bfloat16 or wider, within the bound.
A program may use at most 64 MiB of HBM per device.

```python
import math
import jax
import jax.numpy as jnp
from jax import lax

D = 6144
DH = 128
HALF_HEADS = 8
TOK_DEV = 128
SEQUENCE_LENGTH = 512
SEQUENCE_COUNT = 4


def draw_log_decay(key, part):
    random_key_splits = jax.random.split(key, 7)
    fast_share = 5
    fast_heads = jax.random.randint(random_key_splits[0], (HALF_HEADS,), 0, 10) < fast_share
    fast_rate = jnp.exp(jax.random.uniform(random_key_splits[1], (HALF_HEADS,), jnp.float32, math.log(2.5 / TOK_DEV), math.log(4.0 / TOK_DEV)))
    slow_rate = jnp.exp(jax.random.uniform(random_key_splits[2], (HALF_HEADS,), jnp.float32, math.log(0.05 / SEQUENCE_LENGTH), math.log(0.4 / SEQUENCE_LENGTH)))
    head_decay_speed = jnp.where(fast_heads, fast_rate, slow_rate)
    jitter_level = jnp.exp(jax.random.uniform(random_key_splits[3], (SEQUENCE_COUNT, SEQUENCE_LENGTH, HALF_HEADS), jnp.float32, -math.log(2.0), math.log(2.0)))
    block_multiplier = jnp.exp(jax.random.uniform(random_key_splits[4], (SEQUENCE_COUNT, SEQUENCE_LENGTH // TOK_DEV, 1, HALF_HEADS), jnp.float32, -math.log(2.0), math.log(2.0)))
    block_multiplier = jnp.broadcast_to(block_multiplier, (SEQUENCE_COUNT, SEQUENCE_LENGTH // TOK_DEV, TOK_DEV, HALF_HEADS)).reshape(SEQUENCE_COUNT, SEQUENCE_LENGTH, HALF_HEADS)
    spike_positions = jax.random.randint(random_key_splits[5], (SEQUENCE_COUNT, 3), 0, SEQUENCE_LENGTH)
    spike_mask = jnp.any(jnp.arange(SEQUENCE_LENGTH)[None, :, None] == spike_positions[:, None, :], axis=2)
    spike_strength = jax.random.uniform(random_key_splits[6], (SEQUENCE_COUNT, SEQUENCE_LENGTH, HALF_HEADS), jnp.float32, math.log(0.6), math.log(0.8))
    return -head_decay_speed[None, None, :] * jitter_level * block_multiplier + jnp.where(spike_mask[:, :, None], spike_strength, 0.0)


def spiked(entries, stream_key, source, target, parts, factor):
    def block_of(dim):
        return (jnp.arange(entries.shape[dim]) // (entries.shape[dim] // parts)).reshape((-1,) + (1,) * (entries.ndim - 1 - dim))

    near = jax.random.permutation(stream_key, parts)[block_of(target)]
    second = (block_of(target) + parts // 2) % parts
    return jnp.where((block_of(source) == near) | (block_of(source) == second), factor * entries, entries)


def block_levels(stream_key, shape, cuts, smallest, top_value):
    def one(axis_at, blocks):
        draws = jax.random.uniform(jax.random.fold_in(jax.random.fold_in(stream_key, 6), axis_at), (blocks,), jnp.float32, smallest / len(cuts), top_value / len(cuts))
        return jnp.repeat(jnp.exp(draws), shape[axis_at] // blocks).reshape((-1,) + (1,) * (len(shape) - axis_at - 1))

    level = one(*cuts[0])
    for cut in cuts[1:]:
        level = level * one(*cut)
    return level


def centred(rng, dims, deviation, most, cuts=(), kind=jnp.bfloat16):
    drawn = deviation * jax.random.normal(rng, dims, jnp.float32)
    if cuts:
        drawn = drawn * block_levels(rng, dims, cuts, -0.22, 0.18)
    return jnp.clip(drawn, -most, most).astype(kind)


def bell_draw_with(own_key, shape, deviation, most, cuts, heavy, kind=jnp.bfloat16):
    result = deviation * jax.random.normal(own_key, shape, jnp.float32)
    if cuts:
        result = result * block_levels(own_key, shape, cuts, -0.22, 0.18)
    return jnp.clip(spiked(result, jax.random.fold_in(own_key, 3), *heavy), -most, most).astype(kind)


def setup_inputs(seed: int = 0) -> dict:
    keys = jax.random.split(jax.random.key(seed), 7)
    return {
        "layer_input": bell_draw_with(keys[0], (SEQUENCE_COUNT, SEQUENCE_LENGTH, D), 1.0, 6.0, ((0, 4), (1, 4)), (1, 2, 4, 2.0)),
        "queries": centred(keys[1], (SEQUENCE_COUNT, SEQUENCE_LENGTH, HALF_HEADS * DH), 1.0, 6.0, ((0, 4), (1, 4), (2, 2))),
        "key_rows": centred(keys[2], (SEQUENCE_COUNT, SEQUENCE_LENGTH, HALF_HEADS * DH), 1.0, 6.0, ((0, 4), (1, 4), (2, 2))),
        "value_rows": centred(keys[3], (SEQUENCE_COUNT, SEQUENCE_LENGTH, HALF_HEADS * DH), 1.0, 6.0, ((0, 4), (1, 4), (2, 2))),
        "grad_out": centred(keys[4], (SEQUENCE_COUNT, SEQUENCE_LENGTH, HALF_HEADS * DH), 1.0, 6.0, ((0, 4), (1, 4), (2, 2))),
        "log_decay": draw_log_decay(jax.random.fold_in(keys[6], 71), 0),
    }


top_precision = lax.Precision.HIGHEST

def carry_step(carried, item):
    state, total = item
    return (jnp.exp(total) * carried + state, carried)

def product(form, left, right):
    return jnp.einsum(form, left.astype(jnp.float32), right.astype(jnp.float32), precision=top_precision)

def one_head(inputs):
    query_head, key_head, value_head, grad_head, decay_head = inputs
    blocks = SEQUENCE_LENGTH // TOK_DEV
    query_blocks = query_head.reshape(blocks, TOK_DEV, DH)
    key_blocks = key_head.reshape(blocks, TOK_DEV, DH)
    value_blocks = value_head.reshape(blocks, TOK_DEV, DH)
    grad_blocks = grad_head.reshape(blocks, TOK_DEV, DH)
    running = jnp.cumsum(decay_head.reshape(blocks, TOK_DEV), axis=1)
    totals = running[:, -1]
    positions = jnp.arange(TOK_DEV)
    lower_mask = positions[:, None] >= positions[None, :]
    decay_mask = jnp.where(lower_mask[None], jnp.exp(jnp.minimum(running[:, :, None] - running[:, None, :], 0.0)), 0.0)
    to_end = jnp.exp(totals[:, None] - running)
    from_start = jnp.exp(running)
    key_rows_scaled = (key_blocks * to_end[:, :, None]).astype(jnp.bfloat16)
    scaled_queries = (query_blocks * from_start[:, :, None]).astype(jnp.bfloat16)
    key_state = product('btk,btv->bkv', key_rows_scaled, value_blocks)
    query_state = product('btq,btv->bqv', scaled_queries, grad_blocks)
    empty = jnp.zeros((DH, DH), jnp.float32)
    unused, prefix_running = lax.scan(carry_step, empty, (key_state, totals))
    unused, suffix = lax.scan(carry_step, empty, (query_state, totals), reverse=True)
    prefix_reduced = prefix_running.astype(jnp.bfloat16)
    suffix_low = suffix.astype(jnp.bfloat16)
    value_weights = (product('btv,bjv->btj', grad_blocks, value_blocks) * decay_mask).astype(jnp.bfloat16)
    key_weights = (product('btq,bjq->btj', query_blocks, key_blocks) * decay_mask).astype(jnp.bfloat16)
    scale = 1.0 / DH
    grad_query = (product('btj,bjk->btk', value_weights, key_blocks) + from_start[:, :, None] * product('bkv,btv->btk', prefix_reduced, grad_blocks)) * scale
    grad_key = (product('btj,btq->bjq', value_weights, query_blocks) + to_end[:, :, None] * product('bqv,bjv->bjq', suffix_low, value_blocks)) * scale
    grad_value = (product('btj,btv->bjv', key_weights, grad_blocks) + to_end[:, :, None] * product('bqv,bjq->bjv', suffix_low, key_blocks)) * scale
    return (grad_query.reshape(SEQUENCE_LENGTH, DH), grad_key.reshape(SEQUENCE_LENGTH, DH), grad_value.reshape(SEQUENCE_LENGTH, DH))

def heads_major(array):
    return array.reshape(SEQUENCE_COUNT, SEQUENCE_LENGTH, HALF_HEADS, DH).transpose(0, 2, 1, 3).reshape(SEQUENCE_COUNT * HALF_HEADS, SEQUENCE_LENGTH, DH)

def tokens_major(array):
    return array.reshape(SEQUENCE_COUNT, HALF_HEADS, SEQUENCE_LENGTH, DH).transpose(0, 2, 1, 3).reshape(SEQUENCE_COUNT, SEQUENCE_LENGTH, HALF_HEADS * DH).astype(jnp.bfloat16)

def weight_grad(flat_input, gradient):
    factor = 1.0 / math.sqrt(SEQUENCE_COUNT * SEQUENCE_LENGTH)
    summed = lax.dot_general(flat_input, gradient.reshape(SEQUENCE_COUNT * SEQUENCE_LENGTH, HALF_HEADS * DH), (((0,), (0,)), ((), ())), preferred_element_type=jnp.float32)
    return (summed * factor).astype(jnp.bfloat16)

def reference(layer_input, queries, key_rows, value_rows, grad_out, log_decay):
    decays = log_decay.transpose(0, 2, 1).reshape(SEQUENCE_COUNT * HALF_HEADS, SEQUENCE_LENGTH)
    query_grads, key_grads, value_grads = lax.map(one_head, (heads_major(queries), heads_major(key_rows), heads_major(value_rows), heads_major(grad_out), decays))
    grad_query = tokens_major(query_grads)
    grad_key = tokens_major(key_grads)
    grad_value = tokens_major(value_grads)
    flat_input = layer_input.reshape(SEQUENCE_COUNT * SEQUENCE_LENGTH, D)
    key_weight_grad = weight_grad(flat_input, grad_key)
    value_weight_grad = weight_grad(flat_input, grad_value)
    return (grad_query, grad_key, grad_value, key_weight_grad, value_weight_grad)
```

```python
import functools
import math

import jax
import jax.numpy as jnp
from jax import lax
from jax.experimental import pallas as pl
from jax.experimental.pallas import tpu as pltpu
from jax.sharding import PartitionSpec as P

DH = 128
GROUPS = 2
PIECES = 1
MESH = pl.DeviceIdType.MESH
BF16 = jnp.bfloat16
F32 = jnp.float32


def dot(left, right, dims):
    return lax.dot_general(left, right, (dims, ((), ())), preferred_element_type=F32)


NN = ((1,), (0,))
NT = ((1,), (1,))
TN = ((0,), (0,))


def kernel(
    n, dp, heads, factor,
    x_hbm, q_hbm, k_hbm, v_hbm, g_hbm, ld_hbm,
    gq_ref, gk_ref, gv_ref, ok_ref, ov_ref,
    q_ref, k_ref, v_ref, g_ref, ld_ref,
    qst, kst, suf, pre, suf_out, pre_out, acc_q, acc_k, acc_v,
    x_own, x_far, far_t, own_t, xt, gg, acc,
    in_sem, xl_sem, st_send, st_recv, xc_send, xc_recv, xz_send, xz_recv,
    xx_send, xx_recv, xy_send, xy_recv, gz_send, gz_recv, gx_send, gx_recv,
    gc_send, gc_recv, out_send, out_recv,
):
    s = lax.axis_index("seq")
    d = lax.axis_index("dp")
    head = lax.axis_index("head")
    teams = dp // 2
    team = lax.div(d, 2)
    lo = lax.rem(d, 2)
    side = lax.rem(head, 2)
    mate = head + 1 - 2 * side
    twin = d + 1 - 2 * lo
    hub = lo == side
    length, cols = x_own.shape
    half = cols // 2
    aligned = half % 128 == 0
    piece = half // PIECES
    width = q_ref.shape[1]
    wide = width // GROUPS
    group = heads // GROUPS
    parts = [kind * GROUPS + i for i in range(GROUPS) for kind in range(2)]
    outs = (ok_ref, ov_ref)
    sent = []

    def over(j):
        return lax.div(s + j, n)

    def block(j):
        return s + j - over(j) * (s + 2 * j + 1 - n)

    def source(i):
        return lax.rem(team + teams - i, teams)

    def peer(i):
        return 2 * lax.rem(team + i, teams) + lo

    def start(copy, when=None):
        sent.append((copy, when))
        if when is None:
            copy.start()
        else:
            pl.when(when)(copy.start)

    def remote(src, dst, send_sem, recv_sem, **device):
        return pltpu.make_async_remote_copy(
            src_ref=src, dst_ref=dst, send_sem=send_sem, recv_sem=recv_sem,
            device_id=device, device_id_type=MESH,
        )

    loads = [
        pltpu.make_async_copy(src, dst, in_sem.at[i])
        for i, (src, dst) in enumerate(
            ((ld_hbm, ld_ref), (q_hbm, q_ref), (g_hbm, g_ref), (k_hbm, k_ref), (v_hbm, v_ref))
        )
    ]
    x_loads = [
        pltpu.make_async_copy(
            x_hbm.at[:, pl.ds(pl.multiple_of(s * cols, 128), cols)], x_own, xl_sem.at[0]
        )
    ]
    for j in range(1, n):
        begin = block(j) * cols + (side * half if aligned else 0)
        x_loads.append(
            pltpu.make_async_copy(
                x_hbm.at[:, pl.ds(pl.multiple_of(begin, 128), x_far.shape[2])],
                x_far.at[j - 1], xl_sem.at[j],
            )
        )
    for copy in x_loads + loads:
        copy.start()

    barrier = pltpu.get_barrier_semaphore()

    def greet(**device):
        pl.semaphore_signal(barrier, inc=1, device_id=device, device_id_type=MESH)

    for j in range(1, n):
        greet(seq=lax.rem(s + j, n))
        greet(seq=lax.rem(s + j, n), dp=twin)
    greet(dp=twin)
    for i in range(1, teams):
        greet(dp=peer(i))
    greet(head=mate)

    def x_at(i, j):
        return source(i) * n + block(j)

    x_loads[0].wait()
    other = 1 - lo
    if aligned:
        own_t[...] = x_own[:, pl.ds(pl.multiple_of(other * half, 128), half)].T
        leaving = own_t
    else:
        own_t[...] = x_own[...].T
        leaving = own_t.at[pl.ds(pl.multiple_of(other * half, 16), half)]
    pl.semaphore_wait(barrier, 2 * (n - 1) + 1 + (teams - 1) + 1)
    x_twin = remote(leaving, xt.at[x_at(0, 0), lo], xc_send, xc_recv, dp=twin)
    start(x_twin)
    if aligned:
        xt[x_at(0, 0), lo] = x_own[:, pl.ds(pl.multiple_of(lo * half, 128), half)].T
    else:
        xt[x_at(0, 0), lo] = own_t[pl.ds(pl.multiple_of(lo * half, 16), half), :]

    def x_across(i, j, p):
        at = xt.at[x_at(0, j), :, pl.ds(p * piece, piece)]
        return remote(at, at, xx_send.at[i - 1, j, p], xx_recv.at[i - 1, j, p], dp=peer(i))

    def x_beside(i, j, p):
        at = xt.at[x_at(i, j), :, pl.ds(p * piece, piece)]
        return remote(at, at, xy_send.at[i, j, p], xy_recv.at[i, j, p], head=mate)

    def x_out(j):
        x_loads[j].wait()
        far_t[j - 1] = x_far[j - 1].T
        for p in range(PIECES):
            rows = pl.ds(p * piece, piece)
            begin = p * piece + (0 if aligned else side * half)
            start(
                remote(
                    far_t.at[j - 1, pl.ds(begin, piece)], xt.at[team * n + s, lo, rows],
                    xz_send.at[j - 1, p], xz_recv.at[lo, s, p], seq=block(j), dp=2 * team + side,
                )
            )

    def x_arrive(j):
        for p in range(PIECES):
            if j:
                @pl.when(hub)
                def _():
                    for c in range(2):
                        at = xt.at[x_at(0, j), c, pl.ds(p * piece, piece)]
                        remote(
                            at, at, xz_send.at[0, p], xz_recv.at[c, block(j), p], dp=twin
                        ).wait_recv()
            for i in range(1, teams):
                start(x_across(i, j, p), hub)
            if j:
                start(x_beside(0, j, p), hub)

    def x_relay(j):
        for i in range(1, teams):
            for p in range(PIECES):
                @pl.when(hub)
                def _():
                    x_across(i, j, p).wait_recv()

                start(x_beside(i, j, p), hub)

    def x_need(i, j):
        if i or j:
            for p in range(PIECES):
                @pl.when(jnp.logical_not(hub))
                def _():
                    x_beside(i, j, p).wait_recv()

    x_out(1)
    x_twin.wait_recv()
    x_arrive(0)
    for j in range(2, n):
        x_out(j)

    row = lax.broadcasted_iota(jnp.int32, (length, length), 0)
    col = lax.broadcasted_iota(jnp.int32, (length, length), 1)
    lower = row >= col
    tri = jnp.where(lower, 1.0, 0.0).astype(F32)
    loads[0].wait()
    decays = ld_ref[...]
    exact = lax.Precision.HIGHEST
    cum = lax.dot_general(tri, decays, (NT, ((), ())), precision=exact, preferred_element_type=F32)
    cum_row = lax.dot_general(
        decays, tri, (NT, ((), ())), precision=exact, preferred_element_type=F32
    )
    total = cum[length - 1 : length, :]
    from_start = jnp.exp(cum)
    to_end = jnp.exp(total - cum)
    carry = jnp.exp(total)

    def spread(columns, h):
        return jnp.broadcast_to(columns[:, h : h + 1], (length, DH))

    def suf_send(h):
        return remote(
            suf_out.at[h], suf.at[h], st_send.at[0, h], st_recv.at[0, h], seq=lax.rem(s + n - 1, n)
        )

    def pre_send(h):
        return remote(
            pre_out.at[h], pre.at[h], st_send.at[1, h], st_recv.at[1, h], seq=lax.rem(s + 1, n)
        )

    first, last = s == 0, s == n - 1
    middle = jnp.logical_and(s > 0, s < n - 1)

    @pl.when(last)
    def _():
        suf[...] = jnp.zeros_like(suf)

    @pl.when(first)
    def _():
        pre[...] = jnp.zeros_like(pre)

    loads[1].wait()
    loads[2].wait()
    for h in range(heads):
        at = pl.ds(h * DH, DH)
        queries = (q_ref[:, at].astype(F32) * spread(from_start, h)).astype(BF16)
        state = dot(queries, g_ref[:, at], TN)
        qst[h] = state

        @pl.when(last)
        def _():
            suf_out[h] = state.astype(BF16)
            suf_send(h).start()

    loads[3].wait()
    loads[4].wait()
    for h in range(heads):
        at = pl.ds(h * DH, DH)
        q, k, v, g = q_ref[:, at], k_ref[:, at], v_ref[:, at], g_ref[:, at]
        keys = (k.astype(F32) * spread(to_end, h)).astype(BF16)
        state = dot(keys, v, TN)
        kst[h] = state

        @pl.when(first)
        def _():
            pre_out[h] = state.astype(BF16)
            pre_send(h).start()

        gap = spread(cum, h) - cum_row[h : h + 1, :]
        mask = jnp.where(lower, jnp.exp(jnp.minimum(gap, 0.0)), 0.0)
        value_weights = (dot(g, v, NT) * mask).astype(BF16)
        key_weights = (dot(q, k, NT) * mask).astype(BF16)
        acc_q[:, at] = dot(value_weights, k, NN)
        acc_k[:, at] = dot(value_weights, q, TN)
        acc_v[:, at] = dot(key_weights, g, TN)
        if h == heads // 2 - 1:
            x_arrive(1)

    scale = 1.0 / DH

    def g_at(i, j, c, part):
        first_row = (source(i) * n + block(j)) * 2 * length + c * length
        return gg.at[pl.ds(pl.multiple_of(first_row, 128), length), pl.ds(part * wide, wide)]

    def g_line(part, j, way, to):
        at = g_at(0, j, lo, part)
        return remote(
            at, at, gz_send.at[part, j, way], gz_recv.at[part, block(j)], seq=lax.rem(to + n, n)
        )

    def g_across(part, i, j):
        at = g_at(0, j, lo, part)
        return remote(
            at, at, gx_send.at[part, i - 1, j], gx_recv.at[part, i - 1, j], dp=peer(i)
        )

    def g_twin(part, i, j, c):
        at = g_at(i, j, c, part)
        return remote(at, at, gc_send.at[part, i, j], gc_recv.at[part, i, j], dp=twin)

    def g_out(part):
        start(g_line(part, 0, 0, s - 1), s > 0)
        start(g_line(part, 0, 1, s + 1), s < n - 1)
        for i in range(1, teams):
            start(g_across(part, i, 0))
        start(g_twin(part, 0, 0, lo))

    def g_arrive(part, j):
        to = s - 1 + 2 * over(j)
        copy = g_line(part, j, 0, to)
        copy.wait_recv()
        start(copy, jnp.logical_and(to >= 0, to < n))
        for i in range(1, teams):
            start(g_across(part, i, j))
        start(g_twin(part, 0, j, lo))

    def g_relay(part, j):
        for i in range(1, teams):
            g_across(part, i, j).wait_recv()
            start(g_twin(part, i, j, lo))

    for i in range(GROUPS):
        for h in range(i * group, (i + 1) * group):
            at = pl.ds(h * DH, DH)

            @pl.when(jnp.logical_not(last))
            def _():
                suf_send(h).wait_recv()

            low_suffix = suf[h]

            @pl.when(middle)
            def _():
                state = qst[h] + carry[:, h : h + 1] * suf[h].astype(F32)
                suf_out[h] = state.astype(BF16)
                suf_send(h).start()

            ends = spread(to_end, h)
            result = ((acc_k[:, at] + ends * dot(v_ref[:, at], low_suffix, NT)) * scale).astype(BF16)
            gk_ref[:, at] = result
            rows = pl.ds(pl.multiple_of((team * n + s) * 2 * length + lo * length, 128), length)
            gg[rows, pl.ds(h * DH, DH)] = result
            result = ((acc_v[:, at] + ends * dot(k_ref[:, at], low_suffix, NN)) * scale).astype(BF16)
            gv_ref[:, at] = result
            gg[rows, pl.ds(width + h * DH, DH)] = result
        g_out(i)
        g_out(GROUPS + i)

    def multiply(i, j, part, final=False):
        pair = x_at(i, j)
        left = jnp.concatenate([xt[pair, 0], xt[pair, 1]], axis=1)
        rows = pl.ds(pl.multiple_of(pair * 2 * length, 128), 2 * length)
        columns = pl.ds(part * wide, wide)
        result = dot(left, gg[rows, columns], NN)
        if i or j:
            result = acc[:, columns] + result
        if not final:
            acc[:, columns] = result
            return
        here = outs[part // GROUPS].at[
            pl.ds(pl.multiple_of(lo * half, 16), half), pl.ds((part % GROUPS) * wide, wide)
        ]
        here[...] = (result * factor).astype(BF16)
        copy = remote(here, here, out_send.at[part], out_recv.at[part], dp=twin)
        start(copy)
        finals.append(copy)

    finals = []

    def product(i, j):
        x_need(i, j)
        for part in parts:
            g_twin(part, i, j, 1 - lo).wait_recv()
            multiply(i, j, part, i == teams - 1 and j == n - 1)

    for j in range(2, n):
        if j == 2:
            for part in parts:
                g_arrive(part, 1)
            x_relay(0)
        x_arrive(j)
    if n == 2:
        for part in parts:
            g_arrive(part, 1)
        x_relay(0)
    for h in range(heads):
        at = pl.ds(h * DH, DH)

        @pl.when(jnp.logical_not(first))
        def _():
            pre_send(h).wait_recv()

        @pl.when(middle)
        def _():
            state = kst[h] + carry[:, h : h + 1] * pre[h].astype(F32)
            pre_out[h] = state.astype(BF16)
            pre_send(h).start()

        carried = spread(from_start, h) * dot(g_ref[:, at], pre[h], NT)
        gq_ref[:, at] = ((acc_q[:, at] + carried) * scale).astype(BF16)
    for j in range(2, n):
        x_relay(j - 1)
        for part in parts:
            g_arrive(part, j)
        for part in parts:
            g_relay(part, j - 2)
        product(0, j - 2)
    x_relay(n - 1)
    for part in parts:
        g_relay(part, n - 2)
    product(0, n - 2)
    product(0, n - 1)
    for j in range(n):
        if j == n - 1:
            for part in parts:
                g_relay(part, j)
        for i in range(1, teams):
            product(i, j)

    @pl.when(s > 0)
    def _():
        for h in range(heads):
            suf_send(h).wait_send()

    @pl.when(s < n - 1)
    def _():
        for h in range(heads):
            pre_send(h).wait_send()

    for copy, when in sent:
        if when is None:
            copy.wait_send()
        else:
            pl.when(when)(copy.wait_send)
    for copy in finals:
        copy.wait_recv()


def store(*refs):
    count = (len(refs) - 1) // 2
    copies = [
        pltpu.make_async_copy(refs[i], refs[count + i], refs[-1].at[i]) for i in range(count)
    ]
    for copy in copies:
        copy.start()
    for copy in copies:
        copy.wait()


def per_device(layer_input, queries, key_rows, value_rows, grad_out, log_decay):
    n = lax.axis_size("seq")
    dp = lax.axis_size("dp")
    teams = dp // 2
    length, width = queries.shape[1:]
    heads = log_decay.shape[2]
    features = layer_input.shape[2]
    cols = features // n
    half = cols // 2
    seen = half if half % 128 == 0 else cols
    parts = 2 * GROUPS
    factor = 1.0 / math.sqrt(dp * n * length)
    vmem = pl.BlockSpec(memory_space=pltpu.VMEM)
    hbm = pl.BlockSpec(memory_space=pltpu.HBM)
    dma = pltpu.SemaphoreType.DMA
    tile = (heads, DH, DH)
    operands = [
        pltpu.with_memory_space_constraint(array, pltpu.HBM)
        for array in (
            layer_input[0], queries[0], key_rows[0], value_rows[0], grad_out[0], log_decay[0].T
        )
    ]
    shapes = [jax.ShapeDtypeStruct((length, width), BF16)] * 3 + [
        jax.ShapeDtypeStruct((cols, width), BF16)
    ] * 2
    grads = pl.pallas_call(
        functools.partial(kernel, n, dp, heads, factor),
        out_shape=shapes,
        in_specs=[hbm] * 6,
        out_specs=[vmem] * 5,
        scratch_shapes=[pltpu.VMEM((length, width), BF16)] * 4
        + [pltpu.VMEM((heads, length), F32)]
        + [pltpu.VMEM(tile, F32)] * 2
        + [pltpu.VMEM(tile, BF16)] * 4
        + [pltpu.VMEM((length, width), F32)] * 3
        + [
            pltpu.VMEM((length, cols), BF16),
            pltpu.VMEM((n - 1, length, seen), BF16),
            pltpu.VMEM((n - 1, seen, length), BF16),
            pltpu.VMEM((seen, length), BF16),
            pltpu.VMEM((teams * n, 2, half, length), BF16),
            pltpu.VMEM((teams * n * 2 * length, 2 * width), BF16),
            pltpu.VMEM((half, 2 * width), F32),
            dma((5,)), dma((n,)), dma((2, heads)), dma((2, heads)), dma, dma,
            dma((n - 1, PIECES)), dma((2, n, PIECES)),
            dma((teams - 1, n, PIECES)), dma((teams - 1, n, PIECES)),
            dma((teams, n, PIECES)), dma((teams, n, PIECES)),
            dma((parts, n, 2)), dma((parts, n)),
            dma((parts, teams - 1, n)), dma((parts, teams - 1, n)),
            dma((parts, teams, n)), dma((parts, teams, n)),
            dma((parts,)), dma((parts,)),
        ],
        compiler_params=pltpu.CompilerParams(
            collective_id=0, has_side_effects=True, vmem_limit_bytes=48 << 20
        ),
    )(*operands)
    grads = pl.pallas_call(
        store,
        out_shape=shapes,
        in_specs=[pl.BlockSpec(memory_space=pl.ANY)] * 5,
        out_specs=[hbm] * 5,
        scratch_shapes=[dma((5,))],
    )(*grads)
    return (grads[0][None], grads[1][None], grads[2][None], grads[3], grads[4])


def solution(mesh):
    return jax.shard_map(
        per_device,
        mesh=mesh,
        in_specs=(
            P("dp", "seq", None),
            P("dp", "seq", "head"),
            P("dp", "seq", "head"),
            P("dp", "seq", "head"),
            P("dp", "seq", "head"),
            P("dp", "seq", "head"),
        ),
        out_specs=(
            P("dp", "seq", "head"),
            P("dp", "seq", "head"),
            P("dp", "seq", "head"),
            P("seq", "head"),
            P("seq", "head"),
        ),
        check_vma=False,
    )
```

```python
import functools
import math

import jax
import jax.numpy as jnp
from jax import lax
from jax.experimental import pallas as pl
from jax.experimental.pallas import tpu as pltpu
from jax.sharding import PartitionSpec as P

DH = 128
GROUPS = 2
PIECES = 1
MESH = pl.DeviceIdType.MESH
BF16 = jnp.bfloat16
F32 = jnp.float32


def dot(left, right, dims):
    return lax.dot_general(left, right, (dims, ((), ())), preferred_element_type=F32)


NN = ((1,), (0,))
NT = ((1,), (1,))
TN = ((0,), (0,))


def kernel(
    n, dp, heads, factor,
    x_hbm, q_hbm, k_hbm, v_hbm, g_hbm, ld_hbm,
    gq_ref, gk_ref, gv_ref, ok_ref, ov_ref,
    q_ref, k_ref, v_ref, g_ref, ld_ref,
    qst, kst, suf, pre, suf_out, pre_out, acc_q, acc_k, acc_v,
    x_own, x_far, far_t, own_t, xt, gg, acc,
    in_sem, xl_sem, st_send, st_recv, xc_send, xc_recv, xz_send, xz_recv,
    xx_send, xx_recv, xy_send, xy_recv, gz_send, gz_recv, gx_send, gx_recv,
    gc_send, gc_recv, out_send, out_recv,
):
    s = lax.axis_index("seq")
    d = lax.axis_index("dp")
    head = lax.axis_index("head")
    teams = dp // 2
    team = lax.div(d, 2)
    lo = lax.rem(d, 2)
    side = lax.rem(head, 2)
    mate = head + 1 - 2 * side
    twin = d + 1 - 2 * lo
    hub = lo == side
    length, cols = x_own.shape
    half = cols // 2
    aligned = half % 128 == 0
    piece = half // PIECES
    width = q_ref.shape[1]
    wide = width // GROUPS
    group = heads // GROUPS
    parts = [kind * GROUPS + i for i in range(GROUPS) for kind in range(2)]
    outs = (ok_ref, ov_ref)
    sent = []

    def over(j):
        return lax.div(s + j, n)

    def block(j):
        return s + j - over(j) * (s + 2 * j + 1 - n)

    def source(i):
        return lax.rem(team + teams - i, teams)

    def peer(i):
        return 2 * lax.rem(team + i, teams) + lo

    def start(copy, when=None):
        sent.append((copy, when))
        if when is None:
            copy.start()
        else:
            pl.when(when)(copy.start)

    def remote(src, dst, send_sem, recv_sem, **device):
        return pltpu.make_async_remote_copy(
            src_ref=src, dst_ref=dst, send_sem=send_sem, recv_sem=recv_sem,
            device_id=device, device_id_type=MESH,
        )

    loads = [
        pltpu.make_async_copy(src, dst, in_sem.at[i])
        for i, (src, dst) in enumerate(
            ((ld_hbm, ld_ref), (q_hbm, q_ref), (g_hbm, g_ref), (k_hbm, k_ref), (v_hbm, v_ref))
        )
    ]
    x_loads = [
        pltpu.make_async_copy(
            x_hbm.at[:, pl.ds(pl.multiple_of(s * cols, 128), cols)], x_own, xl_sem.at[0]
        )
    ]
    for j in range(1, n):
        begin = block(j) * cols + (side * half if aligned else 0)
        x_loads.append(
            pltpu.make_async_copy(
                x_hbm.at[:, pl.ds(pl.multiple_of(begin, 128), x_far.shape[2])],
                x_far.at[j - 1], xl_sem.at[j],
            )
        )
    for copy in x_loads + loads:
        copy.start()

    barrier = pltpu.get_barrier_semaphore()

    def greet(**device):
        pl.semaphore_signal(barrier, inc=1, device_id=device, device_id_type=MESH)

    for j in range(1, n):
        greet(seq=lax.rem(s + j, n))
        greet(seq=lax.rem(s + j, n), dp=twin)
    greet(dp=twin)
    for i in range(1, teams):
        greet(dp=peer(i))
    greet(head=mate)

    def x_at(i, j):
        return source(i) * n + block(j)

    x_loads[0].wait()
    other = 1 - lo
    if aligned:
        own_t[...] = x_own[:, pl.ds(pl.multiple_of(other * half, 128), half)].T
        leaving = own_t
    else:
        own_t[...] = x_own[...].T
        leaving = own_t.at[pl.ds(pl.multiple_of(other * half, 16), half)]
    pl.semaphore_wait(barrier, 2 * (n - 1) + 1 + (teams - 1) + 1)
    x_twin = remote(leaving, xt.at[x_at(0, 0), lo], xc_send, xc_recv, dp=twin)
    start(x_twin)
    if aligned:
        xt[x_at(0, 0), lo] = x_own[:, pl.ds(pl.multiple_of(lo * half, 128), half)].T
    else:
        xt[x_at(0, 0), lo] = own_t[pl.ds(pl.multiple_of(lo * half, 16), half), :]

    def x_across(i, j, p):
        at = xt.at[x_at(0, j), :, pl.ds(p * piece, piece)]
        return remote(at, at, xx_send.at[i - 1, j, p], xx_recv.at[i - 1, j, p], dp=peer(i))

    def x_beside(i, j, p):
        at = xt.at[x_at(i, j), :, pl.ds(p * piece, piece)]
        return remote(at, at, xy_send.at[i, j, p], xy_recv.at[i, j, p], head=mate)

    def x_out(j):
        x_loads[j].wait()
        far_t[j - 1] = x_far[j - 1].T
        for p in range(PIECES):
            rows = pl.ds(p * piece, piece)
            begin = p * piece + (0 if aligned else side * half)
            start(
                remote(
                    far_t.at[j - 1, pl.ds(begin, piece)], xt.at[team * n + s, lo, rows],
                    xz_send.at[j - 1, p], xz_recv.at[lo, s, p], seq=block(j), dp=2 * team + side,
                )
            )

    def x_arrive(j):
        for p in range(PIECES):
            if j:
                @pl.when(hub)
                def _():
                    for c in range(2):
                        at = xt.at[x_at(0, j), c, pl.ds(p * piece, piece)]
                        remote(
                            at, at, xz_send.at[0, p], xz_recv.at[c, block(j), p], dp=twin
                        ).wait_recv()
            for i in range(1, teams):
                start(x_across(i, j, p), hub)
            if j:
                start(x_beside(0, j, p), hub)

    def x_relay(j):
        for i in range(1, teams):
            for p in range(PIECES):
                @pl.when(hub)
                def _():
                    x_across(i, j, p).wait_recv()

                start(x_beside(i, j, p), hub)

    def x_need(i, j):
        if i or j:
            for p in range(PIECES):
                @pl.when(jnp.logical_not(hub))
                def _():
                    x_beside(i, j, p).wait_recv()

    x_out(1)
    x_twin.wait_recv()
    x_arrive(0)
    for j in range(2, n):
        x_out(j)

    row = lax.broadcasted_iota(jnp.int32, (length, length), 0)
    col = lax.broadcasted_iota(jnp.int32, (length, length), 1)
    lower = row >= col
    tri = jnp.where(lower, 1.0, 0.0).astype(F32)
    loads[0].wait()
    decays = ld_ref[...]
    exact = lax.Precision.HIGHEST
    cum = lax.dot_general(tri, decays, (NT, ((), ())), precision=exact, preferred_element_type=F32)
    cum_row = lax.dot_general(
        decays, tri, (NT, ((), ())), precision=exact, preferred_element_type=F32
    )
    total = cum[length - 1 : length, :]
    from_start = jnp.exp(cum)
    to_end = jnp.exp(total - cum)
    carry = jnp.exp(total)

    def spread(columns, h):
        return jnp.broadcast_to(columns[:, h : h + 1], (length, DH))

    def suf_send(h):
        return remote(
            suf_out.at[h], suf.at[h], st_send.at[0, h], st_recv.at[0, h], seq=lax.rem(s + n - 1, n)
        )

    def pre_send(h):
        return remote(
            pre_out.at[h], pre.at[h], st_send.at[1, h], st_recv.at[1, h], seq=lax.rem(s + 1, n)
        )

    first, last = s == 0, s == n - 1
    middle = jnp.logical_and(s > 0, s < n - 1)

    @pl.when(last)
    def _():
        suf[...] = jnp.zeros_like(suf)

    @pl.when(first)
    def _():
        pre[...] = jnp.zeros_like(pre)

    loads[1].wait()
    loads[2].wait()
    for h in range(heads):
        at = pl.ds(h * DH, DH)
        queries = (q_ref[:, at].astype(F32) * spread(from_start, h)).astype(BF16)
        state = dot(queries, g_ref[:, at], TN)
        qst[h] = state

        @pl.when(last)
        def _():
            suf_out[h] = state.astype(BF16)
            suf_send(h).start()

    loads[3].wait()
    loads[4].wait()
    for h in range(heads):
        at = pl.ds(h * DH, DH)
        q, k, v, g = q_ref[:, at], k_ref[:, at], v_ref[:, at], g_ref[:, at]
        keys = (k.astype(F32) * spread(to_end, h)).astype(BF16)
        state = dot(keys, v, TN)
        kst[h] = state

        @pl.when(first)
        def _():
            pre_out[h] = state.astype(BF16)
            pre_send(h).start()

        gap = spread(cum, h) - cum_row[h : h + 1, :]
        mask = jnp.where(lower, jnp.exp(jnp.minimum(gap, 0.0)), 0.0)
        value_weights = (dot(g, v, NT) * mask).astype(BF16)
        key_weights = (dot(q, k, NT) * mask).astype(BF16)
        acc_q[:, at] = dot(value_weights, k, NN)
        acc_k[:, at] = dot(value_weights, q, TN)
        acc_v[:, at] = dot(key_weights, g, TN)
        if h == heads // 2 - 1:
            x_arrive(1)

    scale = 1.0 / DH

    def g_at(i, j, c, part):
        first_row = (source(i) * n + block(j)) * 2 * length + c * length
        return gg.at[pl.ds(pl.multiple_of(first_row, 128), length), pl.ds(part * wide, wide)]

    def g_line(part, j, way, to):
        at = g_at(0, j, lo, part)
        return remote(
            at, at, gz_send.at[part, j, way], gz_recv.at[part, block(j)], seq=lax.rem(to + n, n)
        )

    def g_across(part, i, j):
        at = g_at(0, j, lo, part)
        return remote(
            at, at, gx_send.at[part, i - 1, j], gx_recv.at[part, i - 1, j], dp=peer(i)
        )

    def g_twin(part, i, j, c):
        at = g_at(i, j, c, part)
        return remote(at, at, gc_send.at[part, i, j], gc_recv.at[part, i, j], dp=twin)

    def g_out(part):
        start(g_line(part, 0, 0, s - 1), s > 0)
        start(g_line(part, 0, 1, s + 1), s < n - 1)
        for i in range(1, teams):
            start(g_across(part, i, 0))
        start(g_twin(part, 0, 0, lo))

    def g_arrive(part, j):
        to = s - 1 + 2 * over(j)
        copy = g_line(part, j, 0, to)
        copy.wait_recv()
        start(copy, jnp.logical_and(to >= 0, to < n))
        for i in range(1, teams):
            start(g_across(part, i, j))
        start(g_twin(part, 0, j, lo))

    def g_relay(part, j):
        for i in range(1, teams):
            g_across(part, i, j).wait_recv()
            start(g_twin(part, i, j, lo))

    for i in range(GROUPS):
        for h in range(i * group, (i + 1) * group):
            at = pl.ds(h * DH, DH)

            @pl.when(jnp.logical_not(last))
            def _():
                suf_send(h).wait_recv()

            low_suffix = suf[h]

            @pl.when(middle)
            def _():
                state = qst[h] + carry[:, h : h + 1] * suf[h].astype(F32)
                suf_out[h] = state.astype(BF16)
                suf_send(h).start()

            ends = spread(to_end, h)
            result = ((acc_k[:, at] + ends * dot(v_ref[:, at], low_suffix, NT)) * scale).astype(BF16)
            gk_ref[:, at] = result
            rows = pl.ds(pl.multiple_of((team * n + s) * 2 * length + lo * length, 128), length)
            gg[rows, pl.ds(h * DH, DH)] = result
            result = ((acc_v[:, at] + ends * dot(k_ref[:, at], low_suffix, NN)) * scale).astype(BF16)
            gv_ref[:, at] = result
            gg[rows, pl.ds(width + h * DH, DH)] = result
        g_out(i)
        g_out(GROUPS + i)

    def multiply(i, j, part, final=False):
        pair = x_at(i, j)
        left = jnp.concatenate([xt[pair, 0], xt[pair, 1]], axis=1)
        rows = pl.ds(pl.multiple_of(pair * 2 * length, 128), 2 * length)
        columns = pl.ds(part * wide, wide)
        result = dot(left, gg[rows, columns], NN)
        if i or j:
            result = acc[:, columns] + result
        if not final:
            acc[:, columns] = result
            return
        here = outs[part // GROUPS].at[
            pl.ds(pl.multiple_of(lo * half, 16), half), pl.ds((part % GROUPS) * wide, wide)
        ]
        here[...] = (result * factor).astype(BF16)
        copy = remote(here, here, out_send.at[part], out_recv.at[part], dp=twin)
        start(copy)
        finals.append(copy)

    finals = []

    def product(i, j):
        x_need(i, j)
        for part in parts:
            g_twin(part, i, j, 1 - lo).wait_recv()
            multiply(i, j, part, i == teams - 1 and j == n - 1)

    for j in range(2, n):
        if j == 2:
            for part in parts:
                g_arrive(part, 1)
            x_relay(0)
        x_arrive(j)
    if n == 2:
        for part in parts:
            g_arrive(part, 1)
        x_relay(0)
    for h in range(heads):
        at = pl.ds(h * DH, DH)

        @pl.when(jnp.logical_not(first))
        def _():
            pre_send(h).wait_recv()

        @pl.when(middle)
        def _():
            state = kst[h] + carry[:, h : h + 1] * pre[h].astype(F32)
            pre_out[h] = state.astype(BF16)
            pre_send(h).start()

        carried = spread(from_start, h) * dot(g_ref[:, at], pre[h], NT)
        gq_ref[:, at] = ((acc_q[:, at] + carried) * scale).astype(BF16)
    for j in range(2, n):
        x_relay(j - 1)
        for part in parts:
            g_arrive(part, j)
        for part in parts:
            g_relay(part, j - 2)
        product(0, j - 2)
    x_relay(n - 1)
    for part in parts:
        g_relay(part, n - 2)
    product(0, n - 2)
    product(0, n - 1)
    for j in range(n):
        if j == n - 1:
            for part in parts:
                g_relay(part, j)
        for i in range(1, teams):
            product(i, j)

    @pl.when(s > 0)
    def _():
        for h in range(heads):
            suf_send(h).wait_send()

    @pl.when(s < n - 1)
    def _():
        for h in range(heads):
            pre_send(h).wait_send()

    for copy, when in sent:
        if when is None:
            copy.wait_send()
        else:
            pl.when(when)(copy.wait_send)
    for copy in finals:
        copy.wait_recv()


def store(*refs):
    count = (len(refs) - 1) // 2
    copies = [
        pltpu.make_async_copy(refs[i], refs[count + i], refs[-1].at[i]) for i in range(count)
    ]
    for copy in copies:
        copy.start()
    for copy in copies:
        copy.wait()


def per_device(layer_input, queries, key_rows, value_rows, grad_out, log_decay):
    n = lax.axis_size("seq")
    dp = lax.axis_size("dp")
    teams = dp // 2
    length, width = queries.shape[1:]
    heads = log_decay.shape[2]
    features = layer_input.shape[2]
    cols = features // n
    half = cols // 2
    seen = half if half % 128 == 0 else cols
    parts = 2 * GROUPS
    factor = 1.0 / math.sqrt(dp * n * length)
    vmem = pl.BlockSpec(memory_space=pltpu.VMEM)
    hbm = pl.BlockSpec(memory_space=pltpu.HBM)
    dma = pltpu.SemaphoreType.DMA
    tile = (heads, DH, DH)
    operands = [
        pltpu.with_memory_space_constraint(array, pltpu.HBM)
        for array in (
            layer_input[0], queries[0], key_rows[0], value_rows[0], grad_out[0], log_decay[0].T
        )
    ]
    shapes = [jax.ShapeDtypeStruct((length, width), BF16)] * 3 + [
        jax.ShapeDtypeStruct((cols, width), BF16)
    ] * 2
    grads = pl.pallas_call(
        functools.partial(kernel, n, dp, heads, factor),
        out_shape=shapes,
        in_specs=[hbm] * 6,
        out_specs=[vmem] * 5,
        scratch_shapes=[pltpu.VMEM((length, width), BF16)] * 4
        + [pltpu.VMEM((heads, length), F32)]
        + [pltpu.VMEM(tile, F32)] * 2
        + [pltpu.VMEM(tile, BF16)] * 4
        + [pltpu.VMEM((length, width), F32)] * 3
        + [
            pltpu.VMEM((length, cols), BF16),
            pltpu.VMEM((n - 1, length, seen), BF16),
            pltpu.VMEM((n - 1, seen, length), BF16),
            pltpu.VMEM((seen, length), BF16),
            pltpu.VMEM((teams * n, 2, half, length), BF16),
            pltpu.VMEM((teams * n * 2 * length, 2 * width), BF16),
            pltpu.VMEM((half, 2 * width), F32),
            dma((5,)), dma((n,)), dma((2, heads)), dma((2, heads)), dma, dma,
            dma((n - 1, PIECES)), dma((2, n, PIECES)),
            dma((teams - 1, n, PIECES)), dma((teams - 1, n, PIECES)),
            dma((teams, n, PIECES)), dma((teams, n, PIECES)),
            dma((parts, n, 2)), dma((parts, n)),
            dma((parts, teams - 1, n)), dma((parts, teams - 1, n)),
            dma((parts, teams, n)), dma((parts, teams, n)),
            dma((parts,)), dma((parts,)),
        ],
        compiler_params=pltpu.CompilerParams(
            collective_id=0, has_side_effects=True, vmem_limit_bytes=48 << 20
        ),
    )(*operands)
    grads = pl.pallas_call(
        store,
        out_shape=shapes,
        in_specs=[vmem] * 5,
        out_specs=[hbm] * 5,
        scratch_shapes=[dma((5,))],
        compiler_params=pltpu.CompilerParams(vmem_limit_bytes=1 << 20),
    )(*[pltpu.with_memory_space_constraint(array, pltpu.VMEM) for array in grads])
    return (grads[0][None], grads[1][None], grads[2][None], grads[3], grads[4])


def solution(mesh):
    return jax.shard_map(
        per_device,
        mesh=mesh,
        in_specs=(
            P("dp", "seq", None),
            P("dp", "seq", "head"),
            P("dp", "seq", "head"),
            P("dp", "seq", "head"),
            P("dp", "seq", "head"),
            P("dp", "seq", "head"),
        ),
        out_specs=(
            P("dp", "seq", "head"),
            P("dp", "seq", "head"),
            P("dp", "seq", "head"),
            P("seq", "head"),
            P("seq", "head"),
        ),
        check_vma=False,
    )
```

```python
import functools
import math

import jax
import jax.numpy as jnp
from jax import lax
from jax.experimental import pallas as pl
from jax.experimental.pallas import tpu as pltpu
from jax.sharding import PartitionSpec as P

DH = 128
GROUPS = 2
PIECES = 2
PLACES = 4
HUB = {
    "own": (0.1, 3.5, 8.2, 11.51),
    "xo": (3.6, 8.36),
    "xa": (0.05, 5.11, 14.0, 18.5),
    "xr": (3.67, 15.0, 23.23, 26.91),
    "pre": (10.2, 23.55),
    "gq": 23.6,
    "po": (24.37, 24.69, 25.53, 28.0),
    "pa": (30.61, 31.0, 31.74, 35.91),
}
REST = {
    "own": (0.05, 2.36, 2.53, 11.36),
    "xo": (0.05, 7.3),
    "ga": (12.55, 18.5, 23.5),
    "gr": (14.0, 19.5, 26.37, 32.0),
    "pre": (8.19, 17.19),
    "gq": 30.5,
    "po": (17.08, 20.32, 26.32, 29.31),
    "pa": (28.0, 28.1, 28.81, 33.48),
}
MESH = pl.DeviceIdType.MESH
BF16 = jnp.bfloat16
F32 = jnp.float32


def dot(left, right, dims):
    return lax.dot_general(left, right, (dims, ((), ())), preferred_element_type=F32)


def ramp(times, j):
    return times[j] if j < len(times) else times[-1] + (j + 1 - len(times)) * (times[-1] - times[-2])


NN = ((1,), (0,))
NT = ((1,), (1,))
TN = ((0,), (0,))


def kernel(
    n, dp, heads, factor,
    x_hbm, q_hbm, k_hbm, v_hbm, g_hbm, ld_hbm,
    gq_ref, gk_ref, gv_ref, ok_ref, ov_ref,
    q_ref, k_ref, v_ref, g_ref, ld_ref,
    qst, kst, suf, pre, suf_out, pre_out, acc_q, acc_k, acc_v,
    x_own, x_far, far_t, own_t, xt, gg, acc,
    in_sem, xl_sem, st_send, st_recv, xc_send, xc_recv, xz_send, xz_recv,
    xx_send, xx_recv, xy_send, xy_recv, gz_send, gz_recv, gx_send, gx_recv,
    gc_send, gc_recv, gt_send, gt_recv, out_send, out_recv,
):
    s = lax.axis_index("seq")
    d = lax.axis_index("dp")
    head = lax.axis_index("head")
    teams = dp // 2
    team = lax.div(d, 2)
    lo = lax.rem(d, 2)
    side = lax.rem(head, 2)
    mate = head + 1 - 2 * side
    twin = d + 1 - 2 * lo
    hub = lo == side
    length, cols = x_own.shape
    half = cols // 2
    aligned = half % 128 == 0
    piece = half // PIECES
    width = q_ref.shape[1]
    wide = width // GROUPS
    group = heads // GROUPS
    parts = [kind * GROUPS + i for i in range(GROUPS) for kind in range(2)]
    outs = (ok_ref, ov_ref)
    sent = []

    room = jnp.minimum(s, n - 1 - s)
    inner = jnp.where(s < n - 1 - s, 1, -1)

    def block(j):
        near = s + (j + 1) // 2 if j % 2 else s - j // 2
        return jnp.where(j <= 2 * room, near, s + inner * (j - room))

    def ahead(j):
        return lax.rem(s + j, n)

    def behind(j):
        return lax.rem(s + n - j, n)

    def source(i):
        return lax.rem(team + teams - i, teams)

    def peer(i):
        return 2 * lax.rem(team + i, teams) + lo

    def start(copy, when=None):
        sent.append((copy, when))
        if when is None:
            copy.start()
        else:
            pl.when(when)(copy.start)

    def remote(src, dst, send_sem, recv_sem, **device):
        return pltpu.make_async_remote_copy(
            src_ref=src, dst_ref=dst, send_sem=send_sem, recv_sem=recv_sem,
            device_id=device, device_id_type=MESH,
        )

    loads = [
        pltpu.make_async_copy(src, dst, in_sem.at[i])
        for i, (src, dst) in enumerate(
            ((ld_hbm, ld_ref), (q_hbm, q_ref), (g_hbm, g_ref), (k_hbm, k_ref), (v_hbm, v_ref))
        )
    ]
    x_loads = [
        pltpu.make_async_copy(
            x_hbm.at[:, pl.ds(pl.multiple_of(s * cols, 128), cols)], x_own, xl_sem.at[0]
        )
    ]
    for j in range(1, n):
        begin = ahead(j) * cols + (side * half if aligned else 0)
        x_loads.append(
            pltpu.make_async_copy(
                x_hbm.at[:, pl.ds(pl.multiple_of(begin, 128), x_far.shape[2])],
                x_far.at[j - 1], xl_sem.at[j],
            )
        )
    for copy in x_loads + loads:
        copy.start()

    barrier = pltpu.get_barrier_semaphore()

    def greet(**device):
        pl.semaphore_signal(barrier, inc=1, device_id=device, device_id_type=MESH)

    for j in range(1, n):
        greet(seq=lax.rem(s + j, n))
        greet(seq=lax.rem(s + j, n), dp=twin)
    greet(dp=twin)
    for i in range(1, teams):
        greet(dp=peer(i))
    greet(head=mate)

    def x_at(i, b):
        return source(i) * n + b

    other = 1 - lo
    if aligned:
        leaving = own_t
    else:
        leaving = own_t.at[pl.ds(pl.multiple_of(other * half, 16), half)]
    x_twin = remote(leaving, xt.at[x_at(0, s), lo], xc_send, xc_recv, dp=twin)

    def x_turn_own():
        x_loads[0].wait()
        here = x_at(0, s)
        if aligned:
            own_t[...] = x_own[:, pl.ds(pl.multiple_of(other * half, 128), half)].T
            xt[here, lo] = x_own[:, pl.ds(pl.multiple_of(lo * half, 128), half)].T
        else:
            own_t[...] = x_own[...].T
            xt[here, lo] = own_t[pl.ds(pl.multiple_of(lo * half, 16), half), :]

    def x_turn(j):
        x_loads[j].wait()
        far_t[j - 1] = x_far[j - 1].T

    def x_over(i, b, p):
        at = xt.at[x_at(0, b), :, pl.ds(p * piece, piece)]
        return remote(at, at, xx_send.at[i - 1, b, p], xx_recv.at[i - 1, b, p], dp=peer(i))

    def x_into(i, b, p):
        at = xt.at[x_at(i, b), :, pl.ds(p * piece, piece)]
        return remote(at, at, xx_send.at[i - 1, b, p], xx_recv.at[i - 1, b, p], dp=peer(i))

    def x_beside(i, b, p):
        at = xt.at[x_at(i, b), :, pl.ds(p * piece, piece)]
        return remote(at, at, xy_send.at[i, b, p], xy_recv.at[i, b, p], head=mate)

    def x_out(j):
        for p in range(PIECES):
            rows = pl.ds(p * piece, piece)
            begin = p * piece + (0 if aligned else side * half)
            start(
                remote(
                    far_t.at[j - 1, pl.ds(begin, piece)], xt.at[team * n + s, lo, rows],
                    xz_send.at[j - 1, p], xz_recv.at[lo, s, p], seq=ahead(j), dp=2 * team + side,
                )
            )

    def x_arrive(j):
        b = behind(j)
        for p in range(PIECES):
            if j:
                for c in range(2):
                    at = xt.at[x_at(0, b), c, pl.ds(p * piece, piece)]
                    remote(at, at, xz_send.at[0, p], xz_recv.at[c, b, p], dp=twin).wait_recv()
            for i in range(1, teams):
                start(x_over(i, b, p))
            if j:
                start(x_beside(0, b, p))

    def x_relay(j):
        b = behind(j)
        for i in range(1, teams):
            for p in range(PIECES):
                x_into(i, b, p).wait_recv()
                if j:
                    start(x_beside(i, b, p))

    def x_need(i, j):
        for p in range(PIECES):
            if j:
                x_beside(i, block(j), p).wait_recv()
            elif i:
                x_into(i, s, p).wait_recv()

    row = lax.broadcasted_iota(jnp.int32, (length, length), 0)
    col = lax.broadcasted_iota(jnp.int32, (length, length), 1)
    lower = row >= col
    tri = jnp.where(lower, 1.0, 0.0).astype(F32)
    loads[0].wait()
    decays = ld_ref[...]
    exact = lax.Precision.HIGHEST
    cum = lax.dot_general(tri, decays, (NT, ((), ())), precision=exact, preferred_element_type=F32)
    cum_row = lax.dot_general(
        decays, tri, (NT, ((), ())), precision=exact, preferred_element_type=F32
    )
    total = cum[length - 1 : length, :]
    from_start = jnp.exp(cum)
    to_end = jnp.exp(total - cum)
    carry = jnp.exp(total)

    def spread(columns, h):
        return jnp.broadcast_to(columns[:, h : h + 1], (length, DH))

    def suf_send(h):
        return remote(
            suf_out.at[h], suf.at[h], st_send.at[0, h], st_recv.at[0, h], seq=lax.rem(s + n - 1, n)
        )

    def pre_send(h):
        return remote(
            pre_out.at[h], pre.at[h], st_send.at[1, h], st_recv.at[1, h], seq=lax.rem(s + 1, n)
        )

    first, last = s == 0, s == n - 1
    middle = jnp.logical_and(s > 0, s < n - 1)

    @pl.when(last)
    def _():
        suf[...] = jnp.zeros_like(suf)

    @pl.when(first)
    def _():
        pre[...] = jnp.zeros_like(pre)

    loads[1].wait()
    loads[2].wait()
    for h in range(heads):
        at = pl.ds(h * DH, DH)
        queries = (q_ref[:, at].astype(F32) * spread(from_start, h)).astype(BF16)
        state = dot(queries, g_ref[:, at], TN)
        qst[h] = state

        @pl.when(last)
        def _():
            suf_out[h] = state.astype(BF16)

    loads[3].wait()
    loads[4].wait()
    for h in range(heads):
        at = pl.ds(h * DH, DH)
        q, k, v, g = q_ref[:, at], k_ref[:, at], v_ref[:, at], g_ref[:, at]
        keys = (k.astype(F32) * spread(to_end, h)).astype(BF16)
        state = dot(keys, v, TN)
        kst[h] = state

        @pl.when(first)
        def _():
            pre_out[h] = state.astype(BF16)

        gap = spread(cum, h) - cum_row[h : h + 1, :]
        mask = jnp.where(lower, jnp.exp(jnp.minimum(gap, 0.0)), 0.0)
        value_weights = (dot(g, v, NT) * mask).astype(BF16)
        key_weights = (dot(q, k, NT) * mask).astype(BF16)
        acc_q[:, at] = dot(value_weights, k, NN)
        acc_k[:, at] = dot(value_weights, q, TN)
        acc_v[:, at] = dot(key_weights, g, TN)

    scale = 1.0 / DH

    def g_at(i, j, part):
        first_row = (source(i) * n + block(j)) * 2 * length
        return gg.at[pl.ds(pl.multiple_of(first_row, 128), 2 * length), pl.ds(part * wide, wide)]

    def g_one(c, part):
        first_row = (team * n + s) * 2 * length + c * length
        return gg.at[pl.ds(pl.multiple_of(first_row, 128), length), pl.ds(part * wide, wide)]

    def g_line(part, j, way, to):
        at = g_at(0, j, part)
        return remote(
            at, at, gz_send.at[part, j, way], gz_recv.at[part, block(j)], seq=lax.rem(to + n, n)
        )

    def g_over(part, i, j):
        at = g_at(0, j, part)
        return remote(at, at, gx_send.at[part, i - 1, j], gx_recv.at[part, i - 1, j], dp=peer(i))

    def g_into(part, i, j):
        at = g_at(i, j, part)
        return remote(at, at, gx_send.at[part, i - 1, j], gx_recv.at[part, i - 1, j], dp=peer(i))

    def g_twin(part, i, j, c=0):
        at = g_at(i, j, part) if i or j else g_one(c, part)
        return remote(at, at, gc_send.at[part, i, j], gc_recv.at[part, i, j], dp=twin)

    def g_hand(c, part):
        at = g_one(c, part)
        return remote(at, at, gt_send.at[part], gt_recv.at[part], dp=twin)

    def g_own(part):
        return [
            (g_line(part, 0, 0, s - 1), s > 0),
            (g_line(part, 0, 1, s + 1), s < n - 1),
        ] + [(g_over(part, i, 0), None) for i in range(1, teams)]

    def g_go():
        for part in parts:
            g_hand(1 - lo, part).wait_recv()
            for copy, when in g_own(part):
                if when is None:
                    copy.start()
                else:
                    pl.when(when)(copy.start)

    def g_arrive(part, j):
        to = jnp.where(block(j) > s, s - 1, s + 1)
        copy = g_line(part, j, 0, to)
        copy.wait_recv()
        start(copy, jnp.logical_and(to >= 0, to < n))
        for i in range(1, teams):
            start(g_over(part, i, j))
        start(g_twin(part, 0, j))

    def g_relay(part, j):
        for i in range(1, teams):
            g_into(part, i, j).wait_recv()
            start(g_twin(part, i, j))

    def states(h):
        @pl.when(jnp.logical_not(last))
        def _():
            suf_send(h).wait_recv()

        @pl.when(middle)
        def _():
            state = qst[h] + carry[:, h : h + 1] * suf[h].astype(F32)
            suf_out[h] = state.astype(BF16)
            suf_send(h).start()

    def gradients(h):
        at = pl.ds(h * DH, DH)
        low_suffix = suf[h]
        ends = spread(to_end, h)
        rows = pl.ds(pl.multiple_of((team * n + s) * 2 * length + lo * length, 128), length)
        result = ((acc_k[:, at] + ends * dot(v_ref[:, at], low_suffix, NT)) * scale).astype(BF16)
        gk_ref[:, at] = result
        gg[rows, pl.ds(h * DH, DH)] = result
        result = ((acc_v[:, at] + ends * dot(k_ref[:, at], low_suffix, NN)) * scale).astype(BF16)
        gv_ref[:, at] = result
        gg[rows, pl.ds(width + h * DH, DH)] = result

    def own(place, ahead_of, then):
        mine = s == n - 1 - place if place < PLACES - 1 else s <= n - 1 - place

        @pl.when(mine)
        def _():
            for h in range(heads):
                states(h)
            for i in range(GROUPS):
                for h in range(i * group, (i + 1) * group):
                    gradients(h)
                for part in (i, GROUPS + i):
                    ahead_of(part).start()
            then()

    def multiply(i, j, part, final=False):
        pair = x_at(i, block(j))
        left = jnp.concatenate([xt[pair, 0], xt[pair, 1]], axis=1)
        rows = pl.ds(pl.multiple_of(pair * 2 * length, 128), 2 * length)
        columns = pl.ds(part * wide, wide)
        result = dot(left, gg[rows, columns], NN)
        if i or j:
            result = acc[:, columns] + result
        if not final:
            acc[:, columns] = result
            return
        here = outs[part // GROUPS].at[
            pl.ds(pl.multiple_of(lo * half, 16), half), pl.ds((part % GROUPS) * wide, wide)
        ]
        here[...] = (result * factor).astype(BF16)
        copy = remote(here, here, out_send.at[part], out_recv.at[part], dp=twin)
        start(copy)
        finals.append(copy)

    finals = []

    def product(i, j, part, wait):
        wait(i, j, part)
        multiply(i, j, part, i == teams - 1 and j == n - 1)

    def await_gradients(i, j, part):
        g_twin(part, i, j, 1 - lo).wait_recv()

    def await_features(i, j, part):
        if part == parts[0]:
            x_need(i, j)

    def prefixes(place):
        mine = s == place if place < PLACES - 2 else jnp.logical_and(s >= place, s < n - 1)

        @pl.when(mine)
        def _():
            for h in range(heads):
                pre_send(h).wait_recv()
                state = kst[h] + carry[:, h : h + 1] * pre[h].astype(F32)
                pre_out[h] = state.astype(BF16)
                pre_send(h).start()

    def queries_out():
        @pl.when(last)
        def _():
            for h in range(heads):
                pre_send(h).wait_recv()

        for h in range(heads):
            at = pl.ds(h * DH, DH)
            carried = spread(from_start, h) * dot(g_ref[:, at], pre[h], NT)
            gq_ref[:, at] = ((acc_q[:, at] + carried) * scale).astype(BF16)

    def events(plan, ahead_of, then, wait):
        due = [(plan["gq"], queries_out, ())]
        due += [(plan["own"][place], own, (place, ahead_of, then)) for place in range(PLACES)]
        due += [(plan["pre"][k - 1], prefixes, (k,)) for k in range(1, PLACES - 1)]
        for j in range(2, n):
            due.append((ramp(plan["xo"], j - 2), x_out, (j,)))
        for j in range(n):
            for e, part in enumerate(parts):
                late = 0.01 * e
                due.append((ramp(plan["po"], j) + late, product, (0, j, part, wait)))
                for i in range(1, teams):
                    due.append((ramp(plan["pa"], j) + 0.1 * i + late, product, (i, j, part, wait)))
        return due

    def run(due):
        before = len(sent)
        for _, turn, which in sorted(due, key=lambda entry: entry[0]):
            turn(*which)
        return before

    def settle(before):
        for copy, when in sent[before:]:
            if when is None:
                copy.wait_send()
            else:
                pl.when(when)(copy.wait_send)
        for copy in finals:
            copy.wait_recv()
        del sent[before:], finals[:]

    x_turn_own()
    x_turn(1)
    pl.semaphore_wait(barrier, 2 * (n - 1) + 1 + (teams - 1) + 1)
    start(x_twin)

    @pl.when(last)
    def _():
        for h in range(heads):
            suf_send(h).start()

    x_out(1)

    @pl.when(first)
    def _():
        for h in range(heads):
            pre_send(h).start()

    for j in range(2, n):
        x_turn(j)
    x_twin.wait_recv()

    @pl.when(hub)
    def _():
        due = events(HUB, lambda part: g_hand(lo, part), lambda: None, await_gradients)
        for j in range(n):
            due.append((ramp(HUB["xa"], j), x_arrive, (j,)))
            due.append((ramp(HUB["xr"], j), x_relay, (j,)))
        before = run(due)
        for part in parts:
            g_hand(lo, part).wait_send()
        settle(before)

    @pl.when(jnp.logical_not(hub))
    def _():
        before = len(sent)
        for i in range(1, teams):
            for p in range(PIECES):
                start(x_over(i, s, p))
        due = events(REST, lambda part: g_twin(part, 0, 0, lo), g_go, await_features)
        for e, part in enumerate(parts):
            for j in range(1, n):
                due.append((ramp(REST["ga"], j - 1) + 0.01 * e, g_arrive, (part, j)))
            for j in range(n):
                due.append((ramp(REST["gr"], j) + 0.01 * e, g_relay, (part, j)))
        run(due)
        for part in parts:
            g_twin(part, 0, 0, lo).wait_send()
            sent.extend(g_own(part))
        settle(before)

    @pl.when(s > 0)
    def _():
        for h in range(heads):
            suf_send(h).wait_send()

    @pl.when(s < n - 1)
    def _():
        for h in range(heads):
            pre_send(h).wait_send()

    for copy, when in sent:
        if when is None:
            copy.wait_send()
        else:
            pl.when(when)(copy.wait_send)


def store(*refs):
    count = (len(refs) - 1) // 2
    copies = [
        pltpu.make_async_copy(refs[i], refs[count + i], refs[-1].at[i]) for i in range(count)
    ]
    for copy in copies:
        copy.start()
    for copy in copies:
        copy.wait()


def per_device(layer_input, queries, key_rows, value_rows, grad_out, log_decay):
    n = lax.axis_size("seq")
    dp = lax.axis_size("dp")
    teams = dp // 2
    length, width = queries.shape[1:]
    heads = log_decay.shape[2]
    features = layer_input.shape[2]
    cols = features // n
    half = cols // 2
    seen = half if half % 128 == 0 else cols
    parts = 2 * GROUPS
    factor = 1.0 / math.sqrt(dp * n * length)
    vmem = pl.BlockSpec(memory_space=pltpu.VMEM)
    hbm = pl.BlockSpec(memory_space=pltpu.HBM)
    dma = pltpu.SemaphoreType.DMA
    tile = (heads, DH, DH)
    operands = [
        pltpu.with_memory_space_constraint(array, pltpu.HBM)
        for array in (
            layer_input[0], queries[0], key_rows[0], value_rows[0], grad_out[0], log_decay[0].T
        )
    ]
    shapes = [jax.ShapeDtypeStruct((length, width), BF16)] * 3 + [
        jax.ShapeDtypeStruct((cols, width), BF16)
    ] * 2
    grads = pl.pallas_call(
        functools.partial(kernel, n, dp, heads, factor),
        out_shape=shapes,
        in_specs=[hbm] * 6,
        out_specs=[vmem] * 5,
        scratch_shapes=[pltpu.VMEM((length, width), BF16)] * 4
        + [pltpu.VMEM((heads, length), F32)]
        + [pltpu.VMEM(tile, F32)] * 2
        + [pltpu.VMEM(tile, BF16)] * 4
        + [pltpu.VMEM((length, width), F32)] * 3
        + [
            pltpu.VMEM((length, cols), BF16),
            pltpu.VMEM((n - 1, length, seen), BF16),
            pltpu.VMEM((n - 1, seen, length), BF16),
            pltpu.VMEM((seen, length), BF16),
            pltpu.VMEM((teams * n, 2, half, length), BF16),
            pltpu.VMEM((teams * n * 2 * length, 2 * width), BF16),
            pltpu.VMEM((half, 2 * width), F32),
            dma((5,)), dma((n,)), dma((2, heads)), dma((2, heads)), dma, dma,
            dma((n - 1, PIECES)), dma((2, n, PIECES)),
            dma((teams - 1, n, PIECES)), dma((teams - 1, n, PIECES)),
            dma((teams, n, PIECES)), dma((teams, n, PIECES)),
            dma((parts, n, 2)), dma((parts, n)),
            dma((parts, teams - 1, n)), dma((parts, teams - 1, n)),
            dma((parts, teams, n)), dma((parts, teams, n)),
            dma((parts,)), dma((parts,)), dma((parts,)), dma((parts,)),
        ],
        compiler_params=pltpu.CompilerParams(
            collective_id=0, has_side_effects=True, vmem_limit_bytes=48 << 20
        ),
    )(*operands)
    grads = pl.pallas_call(
        store,
        out_shape=shapes,
        in_specs=[vmem] * 5,
        out_specs=[hbm] * 5,
        scratch_shapes=[dma((5,))],
        compiler_params=pltpu.CompilerParams(vmem_limit_bytes=1 << 20),
    )(*[pltpu.with_memory_space_constraint(array, pltpu.VMEM) for array in grads])
    return (grads[0][None], grads[1][None], grads[2][None], grads[3], grads[4])


def solution(mesh):
    return jax.shard_map(
        per_device,
        mesh=mesh,
        in_specs=(
            P("dp", "seq", None),
            P("dp", "seq", "head"),
            P("dp", "seq", "head"),
            P("dp", "seq", "head"),
            P("dp", "seq", "head"),
            P("dp", "seq", "head"),
        ),
        out_specs=(
            P("dp", "seq", "head"),
            P("dp", "seq", "head"),
            P("dp", "seq", "head"),
            P("seq", "head"),
            P("seq", "head"),
        ),
        check_vma=False,
    )
```

```python
import functools
import math

import jax
import jax.numpy as jnp
from jax import lax
from jax.experimental import pallas as pl
from jax.experimental.pallas import tpu as pltpu
from jax.sharding import PartitionSpec as P

DH = 128
GROUPS = 2
PIECES = 2
PLACES = 4
HUB = {
    "own": (0.1, 3.5, 8.2, 11.51),
    "xo": (3.6, 8.36),
    "xa": (0.05, 5.11, 14.0, 18.5),
    "xr": (3.67, 15.0, 23.23, 26.91),
    "pre": (10.2, 23.55),
    "gq": 23.6,
    "po": (24.37, 24.69, 25.53, 28.0),
    "pa": (30.61, 31.0, 31.74, 35.91),
}
REST = {
    "own": (0.05, 2.36, 2.53, 11.36),
    "xo": (0.05, 7.3),
    "ga": (12.55, 18.5, 23.5),
    "gr": (14.0, 19.5, 26.37, 32.0),
    "pre": (8.19, 17.19),
    "gq": 30.5,
    "po": (17.08, 20.32, 26.32, 29.31),
    "pa": (28.0, 28.1, 28.81, 33.48),
}
MESH = pl.DeviceIdType.MESH
BF16 = jnp.bfloat16
F32 = jnp.float32


def dot(left, right, dims):
    return lax.dot_general(left, right, (dims, ((), ())), preferred_element_type=F32)


def ramp(times, j):
    return times[j] if j < len(times) else times[-1] + (j + 1 - len(times)) * (times[-1] - times[-2])


NN = ((1,), (0,))
NT = ((1,), (1,))
TN = ((0,), (0,))


def kernel(
    n, dp, heads, factor,
    x_hbm, q_hbm, k_hbm, v_hbm, g_hbm, ld_hbm,
    gq_ref, gk_ref, gv_ref, ok_ref, ov_ref,
    q_ref, k_ref, v_ref, g_ref, ld_ref,
    qst, kst, suf, pre, suf_out, pre_out, acc_q, acc_k, acc_v,
    x_own, x_far, far_t, own_t, xt, gg, acc,
    in_sem, xl_sem, st_send, st_recv, xc_send, xc_recv, xz_send, xz_recv,
    xx_send, xx_recv, xy_send, xy_recv, gz_send, gz_recv, gx_send, gx_recv,
    gc_send, gc_recv, gt_send, gt_recv, out_send, out_recv,
):
    s = lax.axis_index("seq")
    d = lax.axis_index("dp")
    head = lax.axis_index("head")
    teams = dp // 2
    team = lax.div(d, 2)
    lo = lax.rem(d, 2)
    side = lax.rem(head, 2)
    mate = head + 1 - 2 * side
    twin = d + 1 - 2 * lo
    hub = lo == side
    length, cols = x_own.shape
    half = cols // 2
    aligned = half % 128 == 0
    piece = half // PIECES
    width = q_ref.shape[1]
    wide = width // GROUPS
    group = heads // GROUPS
    parts = [kind * GROUPS + i for i in range(GROUPS) for kind in range(2)]
    outs = (ok_ref, ov_ref)
    sent = []

    room = jnp.minimum(s, n - 1 - s)
    inner = jnp.where(s < n - 1 - s, 1, -1)

    def block(j):
        near = s + (j + 1) // 2 if j % 2 else s - j // 2
        return jnp.where(j <= 2 * room, near, s + inner * (j - room))

    def ahead(j):
        return lax.rem(s + j, n)

    def behind(j):
        return lax.rem(s + n - j, n)

    def source(i):
        return lax.rem(team + teams - i, teams)

    def peer(i):
        return 2 * lax.rem(team + i, teams) + lo

    def start(copy, when=None):
        sent.append((copy, when))
        if when is None:
            copy.start()
        else:
            pl.when(when)(copy.start)

    def remote(src, dst, send_sem, recv_sem, **device):
        return pltpu.make_async_remote_copy(
            src_ref=src, dst_ref=dst, send_sem=send_sem, recv_sem=recv_sem,
            device_id=device, device_id_type=MESH,
        )

    loads = [
        pltpu.make_async_copy(src, dst, in_sem.at[i])
        for i, (src, dst) in enumerate(
            ((ld_hbm, ld_ref), (q_hbm, q_ref), (g_hbm, g_ref), (k_hbm, k_ref), (v_hbm, v_ref))
        )
    ]
    x_loads = [
        pltpu.make_async_copy(
            x_hbm.at[:, pl.ds(pl.multiple_of(s * cols, 128), cols)], x_own, xl_sem.at[0]
        )
    ]
    for j in range(1, n):
        begin = ahead(j) * cols + (side * half if aligned else 0)
        x_loads.append(
            pltpu.make_async_copy(
                x_hbm.at[:, pl.ds(pl.multiple_of(begin, 128), x_far.shape[2])],
                x_far.at[j - 1], xl_sem.at[j],
            )
        )
    for copy in x_loads + loads:
        copy.start()

    barrier = pltpu.get_barrier_semaphore()

    def greet(**device):
        pl.semaphore_signal(barrier, inc=1, device_id=device, device_id_type=MESH)

    for j in range(1, n):
        greet(seq=lax.rem(s + j, n))
        greet(seq=lax.rem(s + j, n), dp=twin)
    greet(dp=twin)
    for i in range(1, teams):
        greet(dp=peer(i))
    greet(head=mate)

    def x_at(i, b):
        return source(i) * n + b

    other = 1 - lo
    if aligned:
        leaving = own_t
    else:
        leaving = own_t.at[pl.ds(pl.multiple_of(other * half, 16), half)]
    x_twin = remote(leaving, xt.at[x_at(0, s), lo], xc_send, xc_recv, dp=twin)

    def x_turn_own():
        x_loads[0].wait()
        here = x_at(0, s)
        if aligned:
            own_t[...] = x_own[:, pl.ds(pl.multiple_of(other * half, 128), half)].T
            xt[here, lo] = x_own[:, pl.ds(pl.multiple_of(lo * half, 128), half)].T
        else:
            own_t[...] = x_own[...].T
            xt[here, lo] = own_t[pl.ds(pl.multiple_of(lo * half, 16), half), :]

    def x_turn(j):
        x_loads[j].wait()
        far_t[j - 1] = x_far[j - 1].T

    def x_over(i, b, p):
        at = xt.at[x_at(0, b), :, pl.ds(p * piece, piece)]
        return remote(at, at, xx_send.at[i - 1, b, p], xx_recv.at[i - 1, b, p], dp=peer(i))

    def x_into(i, b, p):
        at = xt.at[x_at(i, b), :, pl.ds(p * piece, piece)]
        return remote(at, at, xx_send.at[i - 1, b, p], xx_recv.at[i - 1, b, p], dp=peer(i))

    def x_beside(i, b, p):
        at = xt.at[x_at(i, b), :, pl.ds(p * piece, piece)]
        return remote(at, at, xy_send.at[i, b, p], xy_recv.at[i, b, p], head=mate)

    def x_out(j):
        for p in range(PIECES):
            rows = pl.ds(p * piece, piece)
            begin = p * piece + (0 if aligned else side * half)
            start(
                remote(
                    far_t.at[j - 1, pl.ds(begin, piece)], xt.at[team * n + s, lo, rows],
                    xz_send.at[j - 1, p], xz_recv.at[lo, s, p], seq=ahead(j), dp=2 * team + side,
                )
            )

    def x_arrive(j):
        b = behind(j)
        for p in range(PIECES):
            if j:
                for c in range(2):
                    at = xt.at[x_at(0, b), c, pl.ds(p * piece, piece)]
                    remote(at, at, xz_send.at[0, p], xz_recv.at[c, b, p], dp=twin).wait_recv()
            for i in range(1, teams):
                start(x_over(i, b, p))
            if j:
                start(x_beside(0, b, p))

    def x_relay(j):
        b = behind(j)
        for i in range(1, teams):
            for p in range(PIECES):
                x_into(i, b, p).wait_recv()
                if j:
                    start(x_beside(i, b, p))

    def x_need(i, j):
        for p in range(PIECES):
            if j:
                x_beside(i, block(j), p).wait_recv()
            elif i:
                x_into(i, s, p).wait_recv()

    row = lax.broadcasted_iota(jnp.int32, (length, length), 0)
    col = lax.broadcasted_iota(jnp.int32, (length, length), 1)
    lower = row >= col
    tri = jnp.where(lower, 1.0, 0.0).astype(F32)
    loads[0].wait()
    decays = ld_ref[...]
    exact = lax.Precision.HIGHEST
    cum = lax.dot_general(tri, decays, (NT, ((), ())), precision=exact, preferred_element_type=F32)
    cum_row = lax.dot_general(
        decays, tri, (NT, ((), ())), precision=exact, preferred_element_type=F32
    )
    total = cum[length - 1 : length, :]
    from_start = jnp.exp(cum)
    to_end = jnp.exp(total - cum)
    carry = jnp.exp(total)

    def spread(columns, h):
        return jnp.broadcast_to(columns[:, h : h + 1], (length, DH))

    def suf_send(h):
        return remote(
            suf_out.at[h], suf.at[h], st_send.at[0, h], st_recv.at[0, h], seq=lax.rem(s + n - 1, n)
        )

    def pre_send(h):
        return remote(
            pre_out.at[h], pre.at[h], st_send.at[1, h], st_recv.at[1, h], seq=lax.rem(s + 1, n)
        )

    first, last = s == 0, s == n - 1
    middle = jnp.logical_and(s > 0, s < n - 1)

    @pl.when(last)
    def _():
        suf[...] = jnp.zeros_like(suf)

    @pl.when(first)
    def _():
        pre[...] = jnp.zeros_like(pre)

    loads[1].wait()
    loads[2].wait()
    for h in range(heads):
        at = pl.ds(h * DH, DH)
        queries = (q_ref[:, at].astype(F32) * spread(from_start, h)).astype(BF16)
        state = dot(queries, g_ref[:, at], TN)
        qst[h] = state

        @pl.when(last)
        def _():
            suf_out[h] = state.astype(BF16)

    loads[3].wait()
    loads[4].wait()
    for h in range(heads):
        at = pl.ds(h * DH, DH)
        q, k, v, g = q_ref[:, at], k_ref[:, at], v_ref[:, at], g_ref[:, at]
        keys = (k.astype(F32) * spread(to_end, h)).astype(BF16)
        state = dot(keys, v, TN)
        kst[h] = state

        @pl.when(first)
        def _():
            pre_out[h] = state.astype(BF16)

        gap = spread(cum, h) - cum_row[h : h + 1, :]
        mask = jnp.where(lower, jnp.exp(jnp.minimum(gap, 0.0)), 0.0)
        value_weights = (dot(g, v, NT) * mask).astype(BF16)
        key_weights = (dot(q, k, NT) * mask).astype(BF16)
        acc_q[:, at] = dot(value_weights, k, NN)
        acc_k[:, at] = dot(value_weights, q, TN)
        acc_v[:, at] = dot(key_weights, g, TN)

    scale = 1.0 / DH

    def g_at(i, j, part):
        first_row = (source(i) * n + block(j)) * 2 * length
        return gg.at[pl.ds(pl.multiple_of(first_row, 128), 2 * length), pl.ds(part * wide, wide)]

    def g_one(c, part):
        first_row = (team * n + s) * 2 * length + c * length
        return gg.at[pl.ds(pl.multiple_of(first_row, 128), length), pl.ds(part * wide, wide)]

    def g_line(part, j, way, to):
        at = g_at(0, j, part)
        return remote(
            at, at, gz_send.at[part, j, way], gz_recv.at[part, block(j)], seq=lax.rem(to + n, n)
        )

    def g_over(part, i, j):
        at = g_at(0, j, part)
        return remote(at, at, gx_send.at[part, i - 1, j], gx_recv.at[part, i - 1, j], dp=peer(i))

    def g_into(part, i, j):
        at = g_at(i, j, part)
        return remote(at, at, gx_send.at[part, i - 1, j], gx_recv.at[part, i - 1, j], dp=peer(i))

    def g_twin(part, i, j, c=0):
        at = g_at(i, j, part) if i or j else g_one(c, part)
        return remote(at, at, gc_send.at[part, i, j], gc_recv.at[part, i, j], dp=twin)

    def g_hand(c, part):
        at = g_one(c, part)
        return remote(at, at, gt_send.at[part], gt_recv.at[part], dp=twin)

    def g_own(part):
        return [
            (g_line(part, 0, 0, s - 1), s > 0),
            (g_line(part, 0, 1, s + 1), s < n - 1),
        ] + [(g_over(part, i, 0), None) for i in range(1, teams)]

    def g_go():
        for part in parts:
            g_hand(1 - lo, part).wait_recv()
            for copy, when in g_own(part):
                if when is None:
                    copy.start()
                else:
                    pl.when(when)(copy.start)

    def g_arrive(part, j):
        to = jnp.where(block(j) > s, s - 1, s + 1)
        copy = g_line(part, j, 0, to)
        copy.wait_recv()
        start(copy, jnp.logical_and(to >= 0, to < n))
        for i in range(1, teams):
            start(g_over(part, i, j))
        start(g_twin(part, 0, j))

    def g_relay(part, j):
        for i in range(1, teams):
            g_into(part, i, j).wait_recv()
            start(g_twin(part, i, j))

    def states(h):
        @pl.when(jnp.logical_not(last))
        def _():
            suf_send(h).wait_recv()

        @pl.when(middle)
        def _():
            state = qst[h] + carry[:, h : h + 1] * suf[h].astype(F32)
            suf_out[h] = state.astype(BF16)
            suf_send(h).start()

    def gradients(h):
        at = pl.ds(h * DH, DH)
        low_suffix = suf[h]
        ends = spread(to_end, h)
        rows = pl.ds(pl.multiple_of((team * n + s) * 2 * length + lo * length, 128), length)
        result = ((acc_k[:, at] + ends * dot(v_ref[:, at], low_suffix, NT)) * scale).astype(BF16)
        gk_ref[:, at] = result
        gg[rows, pl.ds(h * DH, DH)] = result
        result = ((acc_v[:, at] + ends * dot(k_ref[:, at], low_suffix, NN)) * scale).astype(BF16)
        gv_ref[:, at] = result
        gg[rows, pl.ds(width + h * DH, DH)] = result

    def own(place, ahead_of, then):
        mine = s == n - 1 - place if place < PLACES - 1 else s <= n - 1 - place

        @pl.when(mine)
        def _():
            for h in range(heads):
                states(h)
            for i in range(GROUPS):
                for h in range(i * group, (i + 1) * group):
                    gradients(h)
                for part in (i, GROUPS + i):
                    ahead_of(part).start()
            then()

    def multiply(i, j, part, final=False):
        pair = x_at(i, block(j))
        left = jnp.concatenate([xt[pair, 0], xt[pair, 1]], axis=1)
        rows = pl.ds(pl.multiple_of(pair * 2 * length, 128), 2 * length)
        columns = pl.ds(part * wide, wide)
        result = dot(left, gg[rows, columns], NN)
        if i or j:
            result = acc[:, columns] + result
        if not final:
            acc[:, columns] = result
            return
        here = outs[part // GROUPS].at[
            pl.ds(pl.multiple_of(lo * half, 16), half), pl.ds((part % GROUPS) * wide, wide)
        ]
        here[...] = (result * factor).astype(BF16)
        copy = remote(here, here, out_send.at[part], out_recv.at[part], dp=twin)
        start(copy)
        finals.append(copy)

    finals = []

    def product(i, j, part, wait):
        wait(i, j, part)
        multiply(i, j, part, i == teams - 1 and j == n - 1)

    def await_gradients(i, j, part):
        g_twin(part, i, j, 1 - lo).wait_recv()

    def await_features(i, j, part):
        if part == parts[0]:
            x_need(i, j)

    def prefixes(place):
        mine = s == place if place < PLACES - 2 else jnp.logical_and(s >= place, s < n - 1)

        @pl.when(mine)
        def _():
            for h in range(heads):
                pre_send(h).wait_recv()
                state = kst[h] + carry[:, h : h + 1] * pre[h].astype(F32)
                pre_out[h] = state.astype(BF16)
                pre_send(h).start()

    def queries_out():
        @pl.when(last)
        def _():
            for h in range(heads):
                pre_send(h).wait_recv()

        for h in range(heads):
            at = pl.ds(h * DH, DH)
            carried = spread(from_start, h) * dot(g_ref[:, at], pre[h], NT)
            gq_ref[:, at] = ((acc_q[:, at] + carried) * scale).astype(BF16)

    def events(plan, ahead_of, then, wait):
        due = [(plan["gq"], queries_out, ())]
        due += [(plan["own"][place], own, (place, ahead_of, then)) for place in range(PLACES)]
        due += [(plan["pre"][k - 1], prefixes, (k,)) for k in range(1, PLACES - 1)]
        for j in range(2, n):
            due.append((ramp(plan["xo"], j - 2), x_out, (j,)))
        for j in range(n):
            for e, part in enumerate(parts):
                late = 0.01 * e
                due.append((ramp(plan["po"], j) + late, product, (0, j, part, wait)))
                for i in range(1, teams):
                    due.append((ramp(plan["pa"], j) + 0.1 * i + late, product, (i, j, part, wait)))
        return due

    def run(due):
        before = len(sent)
        for _, turn, which in sorted(due, key=lambda entry: entry[0]):
            turn(*which)
        return before

    def settle(before):
        for copy, when in sent[before:]:
            if when is None:
                copy.wait_send()
            else:
                pl.when(when)(copy.wait_send)
        for copy in finals:
            copy.wait_recv()
        del sent[before:], finals[:]

    x_turn_own()
    for j in range(1, n):
        x_turn(j)
    pl.semaphore_wait(barrier, 2 * (n - 1) + 1 + (teams - 1) + 1)
    start(x_twin)

    @pl.when(last)
    def _():
        for h in range(heads):
            suf_send(h).start()

    x_out(1)

    @pl.when(first)
    def _():
        for h in range(heads):
            pre_send(h).start()

    x_twin.wait_recv()

    @pl.when(hub)
    def _():
        due = events(HUB, lambda part: g_hand(lo, part), lambda: None, await_gradients)
        for j in range(n):
            due.append((ramp(HUB["xa"], j), x_arrive, (j,)))
            due.append((ramp(HUB["xr"], j), x_relay, (j,)))
        before = run(due)
        for part in parts:
            g_hand(lo, part).wait_send()
        settle(before)

    @pl.when(jnp.logical_not(hub))
    def _():
        before = len(sent)
        for i in range(1, teams):
            for p in range(PIECES):
                start(x_over(i, s, p))
        due = events(REST, lambda part: g_twin(part, 0, 0, lo), g_go, await_features)
        for e, part in enumerate(parts):
            for j in range(1, n):
                due.append((ramp(REST["ga"], j - 1) + 0.01 * e, g_arrive, (part, j)))
            for j in range(n):
                due.append((ramp(REST["gr"], j) + 0.01 * e, g_relay, (part, j)))
        run(due)
        for part in parts:
            g_twin(part, 0, 0, lo).wait_send()
            sent.extend(g_own(part))
        settle(before)

    @pl.when(s > 0)
    def _():
        for h in range(heads):
            suf_send(h).wait_send()

    @pl.when(s < n - 1)
    def _():
        for h in range(heads):
            pre_send(h).wait_send()

    for copy, when in sent:
        if when is None:
            copy.wait_send()
        else:
            pl.when(when)(copy.wait_send)


def store(*refs):
    count = (len(refs) - 1) // 2
    copies = [
        pltpu.make_async_copy(refs[i], refs[count + i], refs[-1].at[i]) for i in range(count)
    ]
    for copy in copies:
        copy.start()
    for copy in copies:
        copy.wait()


def per_device(layer_input, queries, key_rows, value_rows, grad_out, log_decay):
    n = lax.axis_size("seq")
    dp = lax.axis_size("dp")
    teams = dp // 2
    length, width = queries.shape[1:]
    heads = log_decay.shape[2]
    features = layer_input.shape[2]
    cols = features // n
    half = cols // 2
    seen = half if half % 128 == 0 else cols
    parts = 2 * GROUPS
    factor = 1.0 / math.sqrt(dp * n * length)
    vmem = pl.BlockSpec(memory_space=pltpu.VMEM)
    hbm = pl.BlockSpec(memory_space=pltpu.HBM)
    dma = pltpu.SemaphoreType.DMA
    tile = (heads, DH, DH)
    operands = [
        pltpu.with_memory_space_constraint(array, pltpu.HBM)
        for array in (
            layer_input[0], queries[0], key_rows[0], value_rows[0], grad_out[0], log_decay[0].T
        )
    ]
    shapes = [jax.ShapeDtypeStruct((length, width), BF16)] * 3 + [
        jax.ShapeDtypeStruct((cols, width), BF16)
    ] * 2
    grads = pl.pallas_call(
        functools.partial(kernel, n, dp, heads, factor),
        out_shape=shapes,
        in_specs=[hbm] * 6,
        out_specs=[vmem] * 5,
        scratch_shapes=[pltpu.VMEM((length, width), BF16)] * 4
        + [pltpu.VMEM((heads, length), F32)]
        + [pltpu.VMEM(tile, F32)] * 2
        + [pltpu.VMEM(tile, BF16)] * 4
        + [pltpu.VMEM((length, width), F32)] * 3
        + [
            pltpu.VMEM((length, cols), BF16),
            pltpu.VMEM((n - 1, length, seen), BF16),
            pltpu.VMEM((n - 1, seen, length), BF16),
            pltpu.VMEM((seen, length), BF16),
            pltpu.VMEM((teams * n, 2, half, length), BF16),
            pltpu.VMEM((teams * n * 2 * length, 2 * width), BF16),
            pltpu.VMEM((half, 2 * width), F32),
            dma((5,)), dma((n,)), dma((2, heads)), dma((2, heads)), dma, dma,
            dma((n - 1, PIECES)), dma((2, n, PIECES)),
            dma((teams - 1, n, PIECES)), dma((teams - 1, n, PIECES)),
            dma((teams, n, PIECES)), dma((teams, n, PIECES)),
            dma((parts, n, 2)), dma((parts, n)),
            dma((parts, teams - 1, n)), dma((parts, teams - 1, n)),
            dma((parts, teams, n)), dma((parts, teams, n)),
            dma((parts,)), dma((parts,)), dma((parts,)), dma((parts,)),
        ],
        compiler_params=pltpu.CompilerParams(
            collective_id=0, has_side_effects=True, vmem_limit_bytes=48 << 20
        ),
    )(*operands)
    grads = pl.pallas_call(
        store,
        out_shape=shapes,
        in_specs=[vmem] * 5,
        out_specs=[hbm] * 5,
        scratch_shapes=[dma((5,))],
        compiler_params=pltpu.CompilerParams(vmem_limit_bytes=1 << 20),
    )(*[pltpu.with_memory_space_constraint(array, pltpu.VMEM) for array in grads])
    return (grads[0][None], grads[1][None], grads[2][None], grads[3], grads[4])


def solution(mesh):
    return jax.shard_map(
        per_device,
        mesh=mesh,
        in_specs=(
            P("dp", "seq", None),
            P("dp", "seq", "head"),
            P("dp", "seq", "head"),
            P("dp", "seq", "head"),
            P("dp", "seq", "head"),
            P("dp", "seq", "head"),
        ),
        out_specs=(
            P("dp", "seq", "head"),
            P("dp", "seq", "head"),
            P("dp", "seq", "head"),
            P("seq", "head"),
            P("seq", "head"),
        ),
        check_vma=False,
    )
```
